128 devices in a mesh: seq: 32 (over x, y, core), head: 4 (over z).
Axes of the slice: x: 4, y: 4, z: 4, core: 2. Of those that a mesh axis runs over, the one named last changes fastest.
Arguments:
- queries: bfloat16 [8192, 5120], P(('seq', 'head')), may hold values from -12 to 12
- keys: bfloat16 [8192, 5120], P(('seq', 'head')), may hold values from -12 to 12
- values: bfloat16 [8192, 5120], P(('seq', 'head')), may hold values from -6 to 6
- out_grad: bfloat16 [8192, 5120], P(('seq', 'head')), may hold values from -6 to 6
- chain_lengths: int32 [64], replicated, may hold values from 1 to 512, 8192 in all
- block_pairs: int32 [64, 4], replicated, may hold values from -1 to 63, as said below
Outputs:
- attn_out: bfloat16 [8192, 5120], P(('seq', 'head'))
- query_grad: bfloat16 [8192, 5120], P(('seq', 'head'))
- key_grad: bfloat16 [8192, 5120], P(('seq', 'head'))
- value_grad: bfloat16 [8192, 5120], P(('seq', 'head'))
The draws below stay inside these ranges and needn't reach their ends.
Inputs may be any that keep to these rules, and one draw needn't show every extreme that they name: `block_pairs`: row q lists the key blocks that query block q attends to. Slot 0 holds q itself; the other live entries are distinct blocks of the same or an adjacent sequence shard of 256 tokens, in no particular order; empty slots hold -1 and follow the live ones. Every row has 2 or more live entries, and in every draw some row has 4.
All inputs are finite; a program needn't handle non-finite values.
Results may differ from the reference program's by a relative error of at most 0.023.
Values may be sent and summed in bfloat16 or wider, within the bound.
A program may use at most 128 MiB of HBM per device.

```python
import math
import jax
import jax.numpy as jnp
import numpy as np
from jax import lax

D = 5120
HEADS = 40
HEAD_SIZE = 128
TOK_DEV = 256
BLOCK_TOKENS = 128
PAIRS = 4
TOKENS = 8192
CHAINS = 64
CHAIN_MOST = 512


def paired_heads(key):
    base = jax.random.fold_in(key, 7)
    streams = jax.random.split(base, 4)
    query_draw = jnp.clip(jax.random.normal(streams[2], (TOKENS, D)), -6.0, 6.0)
    key_draw = jnp.clip(jax.random.normal(streams[3], (TOKENS, D)), -6.0, 6.0)
    return (query_draw, key_draw)


def draw_queries(key, part):
    return paired_heads(key)[0].astype(jnp.bfloat16)


def draw_keys(key, part):
    return paired_heads(key)[1].astype(jnp.bfloat16)


def draw_block_pairs(key, part):
    nshards = TOKENS // TOK_DEV
    per_shard = TOK_DEV // BLOCK_TOKENS
    nblocks = TOKENS // BLOCK_TOKENS
    width = 3 * per_shard
    base = jax.random.fold_in(key, 11)
    streams = jax.random.split(base, 5)
    block_index = jnp.arange(nblocks, dtype=jnp.int32)
    shard_of = block_index // per_shard
    candidate = (shard_of[:, None] - 1) * per_shard + jnp.arange(width, dtype=jnp.int32)[None, :]
    usable = (candidate >= 0) & (candidate < nblocks) & (candidate != block_index[:, None])
    ranking = jax.random.randint(streams[0], (nblocks, width), 0, 1 << 20) * width + jnp.arange(width, dtype=jnp.int32)[None, :]
    ranking = jnp.where(usable, ranking, 1 << 30)
    order = jnp.argsort(ranking, axis=1, stable=True)
    picked = jnp.take_along_axis(candidate, order, axis=1)[:, :PAIRS - 1]
    shard_top = jax.random.randint(streams[1], (nshards,), 3, PAIRS + 1)
    busiest = jax.random.randint(streams[2], (), 0, nshards)
    shard_top = jnp.where(jnp.arange(nshards) == busiest, PAIRS, shard_top)
    row_top = shard_top[shard_of]
    spread = jax.random.randint(streams[3], (nblocks,), 0, 1 << 20)
    counts = 2 + spread % (row_top - 1)
    full_row = jax.random.randint(streams[4], (nshards,), 0, per_shard)
    counts = jnp.where(block_index % per_shard == full_row[shard_of], row_top, counts)
    slot_number = jnp.arange(PAIRS - 1, dtype=jnp.int32)
    others = jnp.where(slot_number[None, :] < (counts - 1)[:, None], picked, -1)
    return jnp.concatenate([block_index[:, None], others], axis=1).astype(jnp.int32)


def levels(rng, dims, cuts, low, top_value):
    gain, own = 1.0, jax.random.fold_in(rng, 6)
    for dim, blocks in cuts:
        draws = jnp.exp(jax.random.uniform(jax.random.fold_in(own, dim), (blocks,), jnp.float32, low / len(cuts), top_value / len(cuts)))
        gain = gain * jnp.repeat(draws, dims[dim] // blocks).reshape([-1 if axis == dim else 1 for axis in range(len(dims))])
    return gain


def profile(number_of, total, bound, lean):
    loads = [(1 << 20) // math.isqrt(standing ** lean) + 1 for standing in range(2, number_of + 1)]
    rest, holding = total - bound - (number_of - 1), [1] * (number_of - 1)
    while rest > 0:
        free = [i for i in range(number_of - 1) if holding[i] < bound]
        pool, budget = sum([loads[i] for i in free]), rest
        for i in free:
            addition = min(bound - holding[i], max(1, budget * loads[i] // pool), rest)
            holding[i] = holding[i] + addition
            rest = rest - addition
    return np.array([bound] + holding)


def uneven(key, count, total, limit, skew):
    if count == 2:
        one = jax.random.randint(key, (), max(1, total - limit), min(limit, total - 1) + 1)
        return jnp.stack([one, total - one])
    tallies = jnp.asarray(profile(count, total, limit, skew), jnp.int32)
    pairs = (count - 1) // 2
    donor, receiver = tallies[1:1 + 2 * pairs:2], tallies[2:2 + 2 * pairs:2]
    margin = jnp.minimum(donor - 1, limit - receiver)
    moved = jax.random.randint(jax.random.fold_in(key, 1), (pairs,), 0, 1 << 20) % (margin + 1)
    tallies = tallies.at[1:1 + 2 * pairs:2].set(donor - moved).at[2:2 + 2 * pairs:2].set(receiver + moved)
    return tallies[jax.random.permutation(jax.random.fold_in(key, 2), count)]


def gaussian(stream_key, dims, scale, limit, cuts=(), held_as=jnp.bfloat16):
    factor_of = levels(stream_key, dims, cuts, -0.22, 0.18) if cuts else 1.0
    values = jax.random.normal(stream_key, dims, jnp.float32) * scale * factor_of
    return jnp.minimum(jnp.maximum(values, -limit), limit).astype(held_as)


def setup_inputs(seed: int = 0) -> dict:
    seeds = jax.random.split(jax.random.key(seed), 7)
    queries = draw_queries(jax.random.fold_in(seeds[6], 71), 0)
    keys = draw_keys(jax.random.fold_in(seeds[6], 71), 0)
    values = gaussian(seeds[2], (TOKENS, D), 1.0, 6.0, ((0, 128),))
    out_grad = gaussian(seeds[3], (TOKENS, D), 1.0, 6.0, ((0, 128),))
    chain_lengths = uneven(seeds[4], CHAINS, TOKENS, CHAIN_MOST, 2).astype(jnp.int32)
    block_pairs = draw_block_pairs(jax.random.fold_in(seeds[6], 71), 0)
    return {"queries": queries, "keys": keys, "values": values, "out_grad": out_grad, "chain_lengths": chain_lengths, "block_pairs": block_pairs}


masked_score = -1e+30
rotary_base = 10000.0

def rotary_tables(position, half_width):
    column_index = jnp.arange(half_width).astype(jnp.float32)
    frequency = jnp.exp(column_index * (-2.0 * math.log(rotary_base) / (2 * half_width)))
    angle = position.astype(jnp.float32)[:, None] * frequency[None, :]
    return (jnp.cos(angle)[:, None, :], jnp.sin(angle)[:, None, :])

def rotate(values_in, cosine, sine_table):
    half_width = values_in.shape[-1] // 2
    first_half = values_in[..., :half_width]
    second_half = values_in[..., half_width:]
    return jnp.concatenate([first_half * cosine - second_half * sine_table, second_half * cosine + first_half * sine_table], axis=-1)

def unrotate(grads_in, cosine, sine_table):
    half_width = grads_in.shape[-1] // 2
    first_half = grads_in[..., :half_width]
    second_half = grads_in[..., half_width:]
    return jnp.concatenate([first_half * cosine + second_half * sine_table, second_half * cosine - first_half * sine_table], axis=-1)

def chain_positions(chain_lengths, token_rows):
    lengths32 = chain_lengths.astype(jnp.int32)
    starts = (jnp.cumsum(lengths32) - lengths32).astype(jnp.int32)
    begins = lax.optimization_barrier(jnp.max(jnp.where(starts[None, :] <= token_rows[:, None], starts[None, :], 0), axis=1))
    return (token_rows - begins).astype(jnp.int32)

def reference(queries, keys, values, out_grad, chain_lengths, block_pairs):
    total = queries.shape[0]
    nblocks = total // BLOCK_TOKENS
    score_scale = 1.0 / math.sqrt(HEAD_SIZE)
    position = chain_positions(chain_lengths, jnp.arange(total, dtype=jnp.int32))
    cosine, sine_table = rotary_tables(position, HEAD_SIZE // 2)
    head_shape = (total, HEADS, HEAD_SIZE)
    query_rot = rotate(queries.reshape(head_shape).astype(jnp.float32), cosine, sine_table).astype(jnp.bfloat16)
    key_rot = rotate(keys.reshape(head_shape).astype(jnp.float32), cosine, sine_table).astype(jnp.bfloat16)
    value_heads = values.reshape(head_shape)
    grad_heads = out_grad.reshape(head_shape)
    key_block_rows = key_rot.reshape(nblocks, BLOCK_TOKENS, HEADS, HEAD_SIZE)
    value_blocks = value_heads.reshape(nblocks, BLOCK_TOKENS, HEADS, HEAD_SIZE)

    def step(carry, block_index):
        key_acc, value_acc = carry
        listed = block_pairs[block_index]
        live_slot = listed >= 0
        safe_slot = jnp.where(live_slot, listed, 0).astype(jnp.int32)
        query_block = lax.dynamic_slice_in_dim(query_rot, block_index * BLOCK_TOKENS, BLOCK_TOKENS, 0).astype(jnp.float32)
        grad_block = lax.dynamic_slice_in_dim(grad_heads, block_index * BLOCK_TOKENS, BLOCK_TOKENS, 0).astype(jnp.float32)
        key_rows = key_block_rows[safe_slot].astype(jnp.float32)
        value_rows = value_blocks[safe_slot].astype(jnp.float32)
        score = jnp.einsum('qhd,pkhd->hqpk', query_block, key_rows) * score_scale
        score = jnp.where(live_slot[None, None, :, None], score, masked_score)
        row_top = lax.optimization_barrier(jnp.max(score, axis=(2, 3), keepdims=True))
        log_total = row_top + jnp.log(lax.optimization_barrier(jnp.sum(jnp.exp(score - row_top), axis=(2, 3), keepdims=True)))
        probability = jnp.exp(score - log_total)
        weights = probability.astype(jnp.bfloat16)
        attention = jnp.einsum('hqpk,pkhd->qhd', weights.astype(jnp.float32), value_rows).astype(jnp.bfloat16)
        row_delta = lax.optimization_barrier(jnp.sum(grad_block * attention.astype(jnp.float32), axis=-1))
        grad_prob = jnp.einsum('qhd,pkhd->hqpk', grad_block, value_rows)
        grad_score = (probability * (grad_prob - row_delta.T[:, :, None, None]) * score_scale).astype(jnp.bfloat16)
        grad_score32 = grad_score.astype(jnp.float32)
        query_grad_rot = jnp.einsum('hqpk,pkhd->qhd', grad_score32, key_rows)
        key_terms = jnp.einsum('hqpk,qhd->pkhd', grad_score32, query_block)
        value_terms = jnp.einsum('hqpk,qhd->pkhd', weights.astype(jnp.float32), grad_block)
        live_weight = live_slot.astype(jnp.float32)[:, None, None, None]
        key_acc = key_acc.at[safe_slot].add(key_terms * live_weight)
        value_acc = value_acc.at[safe_slot].add(value_terms * live_weight)
        return ((key_acc, value_acc), (attention, query_grad_rot))
    empty = jnp.zeros((nblocks, BLOCK_TOKENS, HEADS, HEAD_SIZE), jnp.float32)
    (key_acc, value_acc), (attn_blocks, query_blocks) = lax.scan(step, (empty, empty), jnp.arange(nblocks, dtype=jnp.int32))
    attn_out = attn_blocks.reshape(total, HEADS * HEAD_SIZE)
    query_grad = unrotate(query_blocks.reshape(head_shape), cosine, sine_table).astype(jnp.bfloat16).reshape(total, HEADS * HEAD_SIZE)
    key_grad = unrotate(key_acc.reshape(head_shape), cosine, sine_table).astype(jnp.bfloat16).reshape(total, HEADS * HEAD_SIZE)
    value_grad = value_acc.reshape(total, HEADS * HEAD_SIZE).astype(jnp.bfloat16)
    return (attn_out, query_grad, key_grad, value_grad)
```

```python
import functools
import math

import jax
import jax.numpy as jnp
from jax import lax
from jax.experimental import pallas as pl
from jax.experimental.pallas import tpu as pltpu
from jax.sharding import PartitionSpec as P

HEAD_SIZE = 128
BLOCK_TOKENS = 128
SCALE = 1.0 / math.sqrt(HEAD_SIZE)
MASKED = -1e30
ROTARY_BASE = 10000.0


def shifted(block, axis, distance):
    devices = lax.axis_size(axis)
    route = [(i, i + distance) for i in range(devices) if 0 <= i + distance < devices]
    return lax.ppermute(block, axis, route)


def chain_positions(chain_lengths, token_rows):
    starts = jnp.cumsum(chain_lengths) - chain_lengths
    begins = jnp.max(jnp.where(starts[None, :] <= token_rows[:, None], starts[None, :], 0), axis=1)
    return token_rows - begins


def rotary_tables(position):
    half = HEAD_SIZE // 2
    column_index = jnp.arange(half).astype(jnp.float32)
    frequency = jnp.exp(column_index * (-2.0 * math.log(ROTARY_BASE) / HEAD_SIZE))
    angle = position.astype(jnp.float32)[:, None] * frequency[None, :]
    cosine, sine = jnp.cos(angle), jnp.sin(angle)
    return (
        jnp.concatenate([cosine, cosine], axis=1),
        jnp.concatenate([-sine, sine], axis=1),
    )


def dot(a, b, dims):
    return lax.dot_general(a, b, (dims, ((), ())), preferred_element_type=jnp.float32)


def attend(bias, cosine, sine, qg, own, low, high, out_qg, out_own, out_low, out_high):
    length = qg.shape[1]
    window = 3 * length

    def rotate(x, start):
        x = x.astype(jnp.float32)
        rows = pl.ds(start, length)
        return x * cosine[rows, :] + pltpu.roll(x, HEAD_SIZE // 2, 1) * sine[rows, :]

    def unrotate(g, start):
        rows = pl.ds(start, length)
        return g * cosine[rows, :] - pltpu.roll(g, HEAD_SIZE // 2, 1) * sine[rows, :]

    query = rotate(qg[0], length).astype(jnp.bfloat16)
    grad = qg[1]
    parts = (low, own, high)
    key = jnp.concatenate(
        [rotate(ref[0], i * length).astype(jnp.bfloat16) for i, ref in enumerate(parts)], axis=0
    )
    value = jnp.concatenate([ref[1] for ref in parts], axis=0)
    blocks = window // BLOCK_TOKENS
    score = dot(key, query, ((1,), (1,))) * SCALE
    score = score.reshape(blocks, BLOCK_TOKENS, length) + bias[:blocks, :][:, None, :]
    score = score.reshape(window, length)
    top = jnp.max(score, axis=0, keepdims=True)
    raised = jnp.exp(score - top)
    probability = raised * (1.0 / jnp.sum(raised, axis=0, keepdims=True))
    weights = probability.astype(jnp.bfloat16)
    attention = dot(value, weights, ((0,), (0,))).T.astype(jnp.bfloat16)
    out_qg[0] = attention
    delta = jnp.sum(
        (grad.astype(jnp.float32) * attention.astype(jnp.float32)).T, axis=0, keepdims=True
    )
    grad_prob = dot(value, grad, ((1,), (1,)))
    grad_score = (probability * (grad_prob - delta) * SCALE).astype(jnp.bfloat16)
    query_grad = dot(key, grad_score, ((0,), (0,))).T
    out_qg[1] = unrotate(query_grad, length).astype(jnp.bfloat16)
    key_grad = dot(grad_score, query, ((1,), (0,)))
    value_grad = dot(weights, grad, ((1,), (0,)))
    for i, ref in enumerate((out_low, out_own, out_high)):
        rows = slice(i * length, (i + 1) * length)
        ref[0] = unrotate(key_grad[rows], i * length).astype(ref.dtype)
        ref[1] = value_grad[rows].astype(ref.dtype)


def attention_kernel(bias, cosine, sine, qg, own, low, high):
    _, length, width = qg.shape
    heads = width // HEAD_SIZE
    whole = lambda a: pl.BlockSpec(a.shape, lambda h: (0, 0))
    column = pl.BlockSpec((2, length, HEAD_SIZE), lambda h: (0, 0, h))
    shape = lambda t: jax.ShapeDtypeStruct((2, length, width), t)
    return pl.pallas_call(
        attend,
        grid=(heads,),
        in_specs=[whole(bias), whole(cosine), whole(sine), column, column, column, column],
        out_specs=[column] * 4,
        out_shape=[shape(t) for t in (jnp.bfloat16, jnp.float32, jnp.bfloat16, jnp.bfloat16)],
        compiler_params=pltpu.CompilerParams(vmem_limit_bytes=48 * 1024 * 1024),
        cost_estimate=pl.CostEstimate(
            flops=12 * heads * 3 * length * length * HEAD_SIZE,
            bytes_accessed=22 * length * width * 2,
            transcendentals=heads * 3 * length * length,
        ),
    )(bias, cosine, sine, qg, own, low, high)


def window_tables(chain_lengths, block_pairs, length):
    shard = lax.axis_index("seq")
    nblk = length // BLOCK_TOKENS
    rows = (shard - 1) * length + jnp.arange(3 * length, dtype=jnp.int32)
    cosine, sine = rotary_tables(chain_positions(chain_lengths, rows))
    listed = lax.dynamic_slice_in_dim(block_pairs, shard * nblk, nblk, 0)
    spot = jnp.where(listed >= 0, listed - (shard - 1) * nblk, -1)
    hits = spot[:, None, :] == jnp.arange(8, dtype=jnp.int32)[None, :, None]
    count = jnp.sum(hits.astype(jnp.float32), axis=2)
    bias = jnp.where(count > 0, jnp.log(jnp.maximum(count, 1.0)), MASKED)
    return jnp.repeat(bias.T, BLOCK_TOKENS, axis=1), cosine, sine


def on_device(queries, keys, values, out_grad, chain_lengths, block_pairs):
    swap_in = functools.partial(
        lax.all_to_all, axis_name="head", split_axis=2, concat_axis=1, tiled=True
    )
    swap_out = functools.partial(
        lax.all_to_all, axis_name="head", split_axis=1, concat_axis=2, tiled=True
    )
    own = swap_in(jnp.stack([keys, values]))
    length = own.shape[1]
    low, high = shifted(own, "seq", 1), shifted(own, "seq", -1)
    qg = swap_in(jnp.stack([queries, out_grad]))
    tables = window_tables(chain_lengths, block_pairs, length)
    out_qg, out_own, out_low, out_high = attention_kernel(*tables, qg, own, low, high)
    from_upper, from_lower = shifted(out_low, "seq", -1), shifted(out_high, "seq", 1)
    done_qg = swap_out(out_qg)
    total = out_own + from_upper.astype(jnp.float32) + from_lower.astype(jnp.float32)
    done_kv = swap_out(total.astype(jnp.bfloat16))
    return done_qg[0], done_qg[1], done_kv[0], done_kv[1]


def solution(mesh):
    rows = P(("seq", "head"), None)
    return jax.shard_map(
        on_device,
        mesh=mesh,
        in_specs=(rows, rows, rows, rows, P(), P()),
        out_specs=(rows, rows, rows, rows),
        check_vma=False,
    )
```
